256 devices in a mesh: seq: 32 (over y, z), dp: 8 (over x, core).
Axes of the slice: x: 4, y: 4, z: 8, core: 2. Of those that a mesh axis runs over, the one named last changes fastest.
Arguments:
- queries: bfloat16 [8, 2048, 16384], P('dp', None, 'seq'), may hold values from -6 to 6
- keys: bfloat16 [8, 2048, 16384], P('dp', None, 'seq'), may hold values from -6 to 6
- values: bfloat16 [8, 2048, 16384], P('dp', None, 'seq'), may hold values from -6 to 6
- random_blocks: int32 [8, 32, 256, 3], P('dp', 'seq'), may hold values from 0 to 255
- global_blocks: int32 [8, 2], P('dp'), may hold values from 0 to 255, as said below
- out_weight: bfloat16 [2048, 2048], P('dp'), may hold values from -0.125 to 0.125
Outputs:
- projected: bfloat16 [8, 16384, 2048], P('dp', 'seq')
The draws below stay inside these ranges and needn't reach their ends.
Inputs may be any that keep to these rules, and one draw needn't show every extreme that they name: `global_blocks`: the two global blocks of a sequence differ; some sequence has block 0 and some has block 255.
All inputs are finite; a program needn't handle non-finite values.
Results may differ from the reference program's by a relative error of at most 0.01.
Values may be sent and summed in bfloat16 or wider, within the bound.
A program may use at most 128 MiB of HBM per device.

```python
import jax
import jax.numpy as jnp
from jax import lax

H = 32
HD = 64
BLK = 64
R = 3
D = 2048
L = 16384
NB = 256
B = 8


def global_choice(key):
    half = NB // 2
    first = jax.random.randint(jax.random.fold_in(key, 777), (B,), 0, half)
    second = jax.random.randint(jax.random.fold_in(key, 778), (B,), half, NB)
    low_item = jax.random.randint(jax.random.fold_in(key, 779), (), 0, B)
    high_item = jax.random.randint(jax.random.fold_in(key, 780), (), 0, B)
    items = jnp.arange(B)
    first = jnp.where(items == low_item, 0, first)
    second = jnp.where(items == high_item, NB - 1, second)
    return jnp.stack([first, second], axis=1).astype(jnp.int32)


def shared_direction(key):
    picks = jax.random.bernoulli(jax.random.fold_in(key, 555), 0.5, (B, D))
    return jnp.where(picks, 1.0, -1.0).astype(jnp.float32)


def base_field(key):
    return jnp.clip(jax.random.normal(key, (B, D, L), jnp.float32), -4.5, 4.5)


def draw_global_blocks(key, part):
    return global_choice(key)


def draw_queries(key, part):
    field = base_field(jax.random.fold_in(key, 11))
    glob = global_choice(key)
    direction = shared_direction(key)
    block_of = (jnp.arange(L) // BLK).astype(jnp.int32)
    in_global = jnp.any(glob[:, :, None] == block_of[None, None, :], axis=1)
    field = jnp.where(in_global[:, None, :], field + direction[:, :, None], field)
    return field.astype(jnp.bfloat16)


def draw_keys(key, part):
    field = base_field(jax.random.fold_in(key, 23))
    direction = shared_direction(key)
    planted_count = 16
    spots = jax.random.randint(jax.random.fold_in(key, 888), (B, planted_count), 0, L)
    weights = jax.random.uniform(jax.random.fold_in(key, 999), (B, planted_count), jnp.float32, 0.8, 1.4)
    hits = spots[:, :, None] == jnp.arange(L)[None, None, :]
    planted = jnp.any(hits, axis=1)
    weight_at = jnp.max(jnp.where(hits, weights[:, :, None], 0.0), axis=1)
    field = jnp.where(planted[:, None, :], weight_at[:, None, :] * direction[:, :, None] + 0.3 * field, field)
    return field.astype(jnp.bfloat16)


def with_ends(values, key, least, largest):
    shape = values.shape
    index_at = [jax.random.randint(jax.random.fold_in(key, axis), (), 0, shape[axis]) for axis in range(len(shape))]
    values = values.at[tuple(index_at)].set(least)
    longest = shape.index(max(shape))
    index_at[longest] = (index_at[longest] + 1) % shape[longest]
    return values.at[tuple(index_at)].set(largest)


def block_levels(key, dims, shards, least, largest):
    gain = 1.0
    for axis_at, parts in shards:
        draws = jax.random.uniform(jax.random.fold_in(jax.random.fold_in(key, 6), axis_at), (parts,), jnp.float32, least / len(shards), largest / len(shards))
        gain = gain * jnp.repeat(jnp.exp(draws), dims[axis_at] // parts).reshape((-1,) + (1,) * (len(dims) - 1 - axis_at))
    return gain


def scatter_about(rng, extent, scale, reach, shards=(), held_as=jnp.bfloat16):
    entries = jax.random.normal(rng, extent, jnp.float32) * scale
    if len(shards) > 0:
        entries = block_levels(rng, extent, shards, -0.22, 0.18) * entries
    return jnp.clip(entries, min=-reach, max=reach).astype(held_as)


def setup_inputs(seed: int = 0) -> dict:
    key_of = jax.random.split(jax.random.key(seed), 7)
    return {
        "queries": draw_queries(jax.random.fold_in(key_of[6], 71), 0),
        "keys": draw_keys(jax.random.fold_in(key_of[6], 71), 0),
        "values": scatter_about(key_of[2], (B, D, L), 1.0, 6.0, ((0, 8), (2, 32))),
        "random_blocks": with_ends(jax.random.randint(key_of[3], (B, H, NB, R), 0, NB), jax.random.fold_in(key_of[3], 1), 0, NB - 1).astype(jnp.int32),
        "global_blocks": draw_global_blocks(jax.random.fold_in(key_of[6], 71), 0),
        "out_weight": scatter_about(key_of[5], (D, D), D ** -0.5, 0.125, ((0, 8),)),
    }


def candidate_blocks(nblocks, glob, rand_h):
    rows = jnp.arange(nblocks, dtype=jnp.int32)
    window = jnp.stack([rows - 1, rows, rows + 1], axis=1)
    globs = jnp.broadcast_to(glob[None, :].astype(jnp.int32), (nblocks, glob.shape[0]))
    cand = jnp.concatenate([window, globs, rand_h.astype(jnp.int32)], axis=1)
    inside = (cand >= 0) & (cand < nblocks)
    width = cand.shape[1]
    equal = cand[:, :, None] == cand[:, None, :]
    earlier = jnp.arange(width)[None, :] < jnp.arange(width)[:, None]
    repeated = jnp.any(equal & earlier[None, :, :], axis=2)
    return jnp.clip(cand, 0, nblocks - 1).astype(jnp.int32), inside & (~repeated)


def head_attention(q_head, k_head, v_head, rand_h, glob):
    length = q_head.shape[1]
    nblocks = length // BLK
    scale = HD ** -0.5
    qb = q_head.astype(jnp.float32).reshape(HD, nblocks, BLK)
    kb = k_head.astype(jnp.float32).reshape(HD, nblocks, BLK)
    vb = v_head.astype(jnp.float32).reshape(HD, nblocks, BLK)
    index, valid = candidate_blocks(nblocks, glob, rand_h)
    kg = jnp.take(kb, index, axis=1)
    vg = jnp.take(vb, index, axis=1)
    scores = jnp.einsum('dnq,dnck->nqck', qb, kg) * scale
    scores = jnp.where(valid[:, None, :, None], scores, -jnp.inf)
    top = jnp.max(scores, axis=(2, 3), keepdims=True)
    expo = jnp.exp(scores - top)
    probs = (expo / jnp.sum(expo, axis=(2, 3), keepdims=True)).astype(jnp.bfloat16)
    sparse = jnp.einsum('nqck,dnck->dnq', probs.astype(jnp.float32), vg)
    qglob = jnp.take(qb, glob, axis=1)
    gscore = jnp.einsum('dgq,dk->gqk', qglob, k_head.astype(jnp.float32)) * scale
    gtop = jnp.max(gscore, axis=2, keepdims=True)
    gexp = jnp.exp(gscore - gtop)
    gprob = (gexp / jnp.sum(gexp, axis=2, keepdims=True)).astype(jnp.bfloat16)
    full = jnp.einsum('gqk,dk->dgq', gprob.astype(jnp.float32), v_head.astype(jnp.float32))
    sparse = sparse.at[:, glob, :].set(full)
    return sparse.astype(jnp.bfloat16).reshape(HD, length)


def reference(queries, keys, values, random_blocks, global_blocks, out_weight):
    batch = queries.shape[0]
    length = queries.shape[2]

    def one_item(item):
        seq_id = item // H
        head_id = item % H
        start = (head_id * HD).astype(jnp.int32)
        q_head = lax.dynamic_slice_in_dim(queries[seq_id], start, HD, 0)
        k_head = lax.dynamic_slice_in_dim(keys[seq_id], start, HD, 0)
        v_head = lax.dynamic_slice_in_dim(values[seq_id], start, HD, 0)
        return head_attention(q_head, k_head, v_head, random_blocks[seq_id, head_id], global_blocks[seq_id])

    heads = lax.map(one_item, jnp.arange(batch * H, dtype=jnp.int32))
    attended = heads.reshape(batch, H * HD, length)

    def project(item):
        return jnp.dot(attended[item].T, out_weight, preferred_element_type=jnp.float32).astype(jnp.bfloat16)

    return lax.map(project, jnp.arange(batch, dtype=jnp.int32))
```

```python
import functools

import jax
import jax.numpy as jnp
from jax import lax
from jax.experimental import pallas as pl
from jax.experimental.pallas import tpu as pltpu
from jax.sharding import PartitionSpec as P

HD = 64
BLK = 64
LANES = 128
CAND = 8
LOG2E = 1.4426950408889634
SCALE = HD ** (-0.5) * LOG2E


def candidate_blocks(nblocks, glob, rand_h):
    rows = jnp.arange(nblocks, dtype=jnp.int32)
    window = jnp.stack([rows - 1, rows, rows + 1], axis=1)
    globs = jnp.broadcast_to(glob[None, :], (nblocks, glob.shape[0]))
    cand = jnp.concatenate([window, globs, rand_h], axis=1)
    inside = (cand >= 0) & (cand < nblocks)
    width = cand.shape[1]
    equal = cand[:, :, None] == cand[:, None, :]
    earlier = jnp.arange(width)[None, :] < jnp.arange(width)[:, None]
    repeated = jnp.any(equal & earlier[None, :, :], axis=2)
    return jnp.clip(cand, 0, nblocks - 1), inside & ~repeated


def rows_of(index, count=BLK):
    return pl.ds(pl.multiple_of(index * count, count), count)


def lane_mask(rows):
    return lax.broadcasted_iota(jnp.int32, (rows, LANES), 1) < HD


def dot_t(a, b):
    return lax.dot_general(a, b, (((1,), (1,)), ((), ())), preferred_element_type=jnp.float32)


def dot_n(a, b):
    return lax.dot_general(a, b, (((1,), (0,)), ((), ())), preferred_element_type=jnp.float32)


def spread(chunk, other):
    return jnp.concatenate([chunk, other], axis=0).T


def sparse_block(block, q_rows, kt, vt, index, bias):
    picks = [rows_of(index[block * CAND + c]) for c in range(CAND)]
    keys = jnp.concatenate([kt[p, :] for p in picks], axis=0)
    scores = dot_t(q_rows, keys) * SCALE
    low = lax.broadcasted_iota(jnp.int32, (1, LANES), 1) < HD
    marks = [
        jnp.where(low, bias[block * CAND + 2 * g], bias[block * CAND + 2 * g + 1])
        for g in range(CAND // 2)
    ]
    scores = scores + jnp.concatenate(marks, axis=1)
    top = jnp.max(scores, axis=1, keepdims=True)
    probs = jnp.exp2(scores - top).astype(jnp.bfloat16)
    vals = jnp.concatenate([vt[p, :] for p in picks], axis=0)
    return dot_n(probs, vals)


def chosen(block, mine, full, glob):
    mine = jnp.where(block == glob[0], full[0:BLK, :], mine)
    return jnp.where(block == glob[1], full[BLK : 2 * BLK, :], mine)


def attend_chunk(chunk, par, out, qt, kt, vt, full, index, bias, glob):
    per = 8
    half = per // 2
    low = lane_mask(BLK)
    for i in range(half):
        first = chunk * per + i + half * par
        second = chunk * per + i + half * (1 - par)
        a = sparse_block(first, qt[rows_of(first), :], kt, vt, index, bias)
        b = sparse_block(second, qt[rows_of(second), :], kt, vt, index, bias)
        a = chosen(first, a, full, glob)
        b = chosen(second, b, full, glob)
        num = jnp.where(low, a, pltpu.roll(b, HD, 1))
        den = jnp.where(low, pltpu.roll(a, HD, 1), b)
        out[i * BLK : (i + 1) * BLK, :] = (num / den).astype(jnp.bfloat16)


def full_blocks(full, qg, kt, vt, held, top):
    turns, _, width = held.shape
    top[...] = jnp.full(top.shape, -jnp.inf, jnp.float32)

    def scores(t, c):
        s = dot_t(qg, kt[rows_of(t, width), :]) * SCALE
        held[t] = s
        best = top[...]
        for g in range(width // LANES):
            best = jnp.maximum(best, s[:, g * LANES : (g + 1) * LANES])
        top[...] = best
        return c

    lax.fori_loop(0, turns, scores, 0)
    best = jnp.max(top[...], axis=1, keepdims=True)
    full[...] = jnp.zeros(full.shape, jnp.float32)

    def values(t, c):
        p = jnp.exp2(held[t] - best).astype(jnp.bfloat16)
        full[...] += dot_n(p, vt[rows_of(t, width), :])
        return c

    lax.fori_loop(0, turns, values, 0)


def attention_kernel(index, bias, glob, q, k, v, out, qt, kt, vt, full, held, top):
    devices, _, width = q.shape
    me = lax.axis_index("seq")
    par = lax.rem(me, 2)

    def turn(s, c):
        rows = rows_of(s, width)
        qt[rows, :] = spread(q[s], q[s])
        kt[rows, :] = spread(k[s], jnp.zeros_like(k[s]))
        vt[rows, :] = spread(v[s], jnp.ones_like(v[s]))
        return c

    lax.fori_loop(0, devices, turn, 0)
    qg = jnp.concatenate([qt[rows_of(glob[0]), :], qt[rows_of(glob[1]), :]], axis=0)
    full_blocks(full, qg, kt, vt, held, top)

    def chunk(s, c):
        attend_chunk(s, par, out.at[s], qt, kt, vt, full, index, bias, glob)
        return c

    lax.fori_loop(0, devices, chunk, 0)


def project_kernel(heads, w, out, total):
    devices, half, _ = heads.shape
    low = lane_mask(half)
    total[...] = jnp.zeros(total.shape, jnp.float32)

    def group(g, c):
        lo, hi, w_lo, w_hi = [], [], [], []
        for p in range(2):
            a, b = heads[4 * g + 2 * p], heads[4 * g + 2 * p + 1]
            lo.append(jnp.where(low, a, b))
            hi.append(jnp.where(low, b, a))
            w_a, w_b = w[rows_of(4 * g + 2 * p), :], w[rows_of(4 * g + 2 * p + 1), :]
            w_lo += [w_a, w_b]
            w_hi += [w_b, w_a]
        total[0:half, :] += dot_n(jnp.concatenate(lo, axis=1), jnp.concatenate(w_lo, axis=0))
        total[half:, :] += dot_n(jnp.concatenate(hi, axis=1), jnp.concatenate(w_hi, axis=0))
        return c

    lax.fori_loop(0, devices // 4, group, 0)
    out[...] = total[...].astype(jnp.bfloat16)


VM = pl.BlockSpec(memory_space=pltpu.VMEM)
SM = pl.BlockSpec(memory_space=pltpu.SMEM)


def attention(index, bias, glob, q, k, v):
    devices, _, width = q.shape
    length = devices * width
    return pl.pallas_call(
        attention_kernel,
        out_shape=jax.ShapeDtypeStruct((devices, width // 2, LANES), jnp.bfloat16),
        in_specs=[SM, SM, SM, VM, VM, VM],
        out_specs=VM,
        scratch_shapes=[
            pltpu.VMEM((length, LANES), jnp.bfloat16),
            pltpu.VMEM((length, LANES), jnp.bfloat16),
            pltpu.VMEM((length, LANES), jnp.bfloat16),
            pltpu.VMEM((2 * BLK, LANES), jnp.float32),
            pltpu.VMEM((devices, 2 * BLK, width), jnp.float32),
            pltpu.VMEM((2 * BLK, LANES), jnp.float32),
        ],
        compiler_params=pltpu.CompilerParams(vmem_limit_bytes=60 << 20),
    )(index, bias, glob, q, k, v)


def project(heads, w):
    devices, half, _ = heads.shape
    return pl.pallas_call(
        project_kernel,
        out_shape=jax.ShapeDtypeStruct((2 * half, w.shape[1]), jnp.bfloat16),
        in_specs=[VM, VM],
        out_specs=VM,
        scratch_shapes=[pltpu.VMEM((2 * half, w.shape[1]), jnp.float32)],
        compiler_params=pltpu.CompilerParams(vmem_limit_bytes=60 << 20),
    )(heads, w)


def local(queries, keys, values, random_blocks, global_blocks, out_weight):
    glob = global_blocks[0]
    width = queries.shape[2]

    def exchange(x):
        return lax.all_to_all(x, "seq", split_axis=0, concat_axis=0, tiled=True)

    k, v, q = (
        exchange(x[0].reshape(-1, HD, width)) for x in (keys, values, queries)
    )
    index, valid = candidate_blocks(random_blocks.shape[2], glob, random_blocks[0, 0])
    bias = jnp.where(valid, 0.0, -jnp.inf).astype(jnp.float32)
    heads = attention(index.reshape(-1), bias.reshape(-1), glob, q, k, v)
    heads = exchange(heads)
    w = lax.all_gather(out_weight, "dp", axis=0, tiled=True)
    return project(heads, w)[None]


def solution(mesh):
    in_specs = (
        P("dp", None, "seq"),
        P("dp", None, "seq"),
        P("dp", None, "seq"),
        P("dp", "seq", None, None),
        P("dp", None),
        P("dp", None),
    )
    out_specs = P("dp", "seq", None)
    return jax.shard_map(local, mesh=mesh, in_specs=in_specs, out_specs=out_specs, check_vma=False)
```

```python
import functools

import jax
import jax.numpy as jnp
from jax import lax
from jax.experimental import pallas as pl
from jax.experimental.pallas import tpu as pltpu
from jax.sharding import PartitionSpec as P

HD = 64
BLK = 64
LANES = 128
CAND = 8
QUAD = 4 * BLK
SCALE = HD ** (-0.5) * 1.4426950408889634
MESH = pl.DeviceIdType.MESH


def candidate_blocks(nblocks, glob, rand_h):
    rows = jnp.arange(nblocks, dtype=jnp.int32)
    window = jnp.stack([rows - 1, rows, rows + 1], axis=1)
    globs = jnp.broadcast_to(glob[None, :], (nblocks, glob.shape[0]))
    cand = jnp.concatenate([window, globs, rand_h], axis=1)
    inside = (cand >= 0) & (cand < nblocks)
    width = cand.shape[1]
    equal = cand[:, :, None] == cand[:, None, :]
    earlier = jnp.arange(width)[None, :] < jnp.arange(width)[:, None]
    repeated = jnp.any(equal & earlier[None, :, :], axis=2)
    return jnp.clip(cand, 0, nblocks - 1), inside & ~repeated


def dot(a, b):
    return lax.dot_general(a, b, (((1,), (0,)), ((), ())), preferred_element_type=jnp.float32)


def lane(shape):
    return lax.broadcasted_iota(jnp.int32, shape, len(shape) - 1)


def low_half(rows):
    return lane((rows, LANES)) < BLK


def swap(x):
    return jnp.concatenate([x[:, BLK:], x[:, :BLK]], axis=1)


def take_query(s, q, qg, glob):
    at = lane((HD, LANES))
    want = jnp.where(at < BLK, glob[0], glob[1])
    kept = qg[...]
    for i in range(q.shape[1] // LANES):
        x = q[:, i * LANES : (i + 1) * LANES]
        first = s * (q.shape[1] // BLK) + 2 * i
        here = first + jnp.where(at < BLK, 0, 1)
        there = first + jnp.where(at < BLK, 1, 0)
        kept = jnp.where(here == want, x, jnp.where(there == want, swap(x), kept))
    qg[...] = kept


def take_key(s, k, kd, qg, held, top):
    per = k.shape[1] // BLK
    tokens = jnp.concatenate([k[...], k[...]], axis=0).T
    for i in range(per):
        kd[s * per + i] = tokens[i * BLK : (i + 1) * BLK, :]
    half = k.shape[1] // 2
    pairs = jnp.where(low_half(half), tokens[:half, :], tokens[half:, :])
    g = qg[...]
    zero = jnp.zeros_like(g)
    weights = jnp.concatenate(
        [jnp.concatenate([g, zero], axis=1), jnp.concatenate([zero, g], axis=1)], axis=0
    )
    scores = dot(pairs, weights) * SCALE
    held[s] = scores
    best = top[...]
    for r in range(half // 8):
        best = jnp.maximum(best, scores[r * 8 : (r + 1) * 8, :])
    top[...] = best


def top_of(top):
    best = jnp.max(top[...], axis=0, keepdims=True)
    best = jnp.maximum(best[:, :LANES], best[:, LANES:])
    return jnp.concatenate([best, best], axis=1)


def take_value(s, v, vd, held, top, full):
    per = v.shape[1] // BLK
    low = low_half(HD)
    for i in range(per // 2):
        x = v[:, i * LANES : (i + 1) * LANES]
        y = swap(x)
        vd[s * per + 2 * i] = jnp.where(low, x, y)
        vd[s * per + 2 * i + 1] = jnp.where(low, y, x)
    half = v.shape[1] // 2
    probs = jnp.exp2(held[s] - top_of(top)).astype(jnp.bfloat16)
    ones = jnp.ones((16, half), jnp.bfloat16)
    lhs = jnp.concatenate([v[:, :half], v[:, half:], ones], axis=0)
    full[...] += dot(lhs, probs)


def finish_full(full, fd):
    num = full[:HD, :LANES] + full[HD : 2 * HD, LANES:]
    row = full[2 * HD : 2 * HD + 1, :]
    out = (num / (row[:, :LANES] + row[:, LANES:])).astype(jnp.bfloat16)
    low = low_half(HD)
    other = swap(out)
    fd[0] = jnp.where(low, out, other)
    fd[1] = jnp.where(low, other, out)


def attend_quad(quad, qq, kd, vd, fd, index, bias, glob):
    low = low_half(BLK)
    base = quad * (4 * CAND)
    at = lane((HD, QUAD)) // BLK
    zero = jnp.zeros_like(qq)
    weights = jnp.concatenate([jnp.where(at == a, qq, zero) for a in range(4)], axis=0)
    picks = [[index[base + a * CAND + c] for c in range(CAND)] for a in range(4)]
    keys = []
    for c in range(CAND):
        k = [kd[picks[a][c]] for a in range(4)]
        keys.append(
            jnp.concatenate([jnp.where(low, k[0], k[1]), jnp.where(low, k[2], k[3])], axis=1)
        )
    scores = dot(jnp.concatenate(keys, axis=0), weights) * SCALE
    marks = bias[quad]
    scores = jnp.concatenate(
        [scores[c * BLK : (c + 1) * BLK, :] + marks[c : c + 1, :] for c in range(CAND)], axis=0
    )
    top = jnp.max(scores, axis=0, keepdims=True)
    probs = jnp.exp2(scores - top).astype(jnp.bfloat16)
    vals = []
    for a in range(4):
        v = [vd[picks[a][c]] for c in range(CAND)]
        vals.append(
            jnp.concatenate(
                [jnp.where(low, v[2 * g], v[2 * g + 1]) for g in range(CAND // 2)], axis=1
            )
        )
    vals.append(jnp.ones((16, CAND * BLK), jnp.bfloat16))
    got = dot(jnp.concatenate(vals, axis=0), probs)
    num = jnp.concatenate(
        [
            jnp.where(low, got[0:64, :LANES], got[64:128, :LANES]),
            jnp.where(low, got[128:192, LANES:], got[192:256, LANES:]),
        ],
        axis=1,
    )
    out = (num / got[256:257, :]).astype(jnp.bfloat16)
    here = quad * 4 + at
    for g in range(2):
        f = fd[g]
        out = jnp.where(here == glob[g], jnp.concatenate([f, f], axis=1), out)
    return out


def tables(glob, rand_h):
    index, valid = candidate_blocks(rand_h.shape[0], glob, rand_h)
    marks = jnp.where(valid, 0.0, -jnp.inf).astype(jnp.float32)
    marks = marks.reshape(-1, 4, CAND).transpose(0, 2, 1)
    return index.reshape(-1), jnp.repeat(marks, BLK, axis=2)


VM = pl.BlockSpec(memory_space=pltpu.VMEM)
SM = pl.BlockSpec(memory_space=pltpu.SMEM)
HB = pl.BlockSpec(memory_space=pl.ANY)

NY = 4
NZ = 8
GROUP = 8


def offset(i):
    a = i // NY
    dz = NZ // 2 + ((a + 1) // 2) * (1 - 2 * lax.rem(a, 2))
    return lax.rem(i + 1, NY), dz


def target(me, i):
    dy, dz = offset(i)
    return lax.rem(me // NZ + dy, NY) * NZ + lax.rem(lax.rem(me, NZ) + dz, NZ)


def source(me, i):
    dy, dz = offset(i)
    return lax.rem(me // NZ + NY - dy, NY) * NZ + lax.rem(lax.rem(me, NZ) + NZ - dz, NZ)


def loop(first, last, f):
    def body(i, c):
        f(i)
        return c

    lax.fori_loop(first, last, body, 0)


def layer_kernel(
    index, glob, bias, q, k, v, w, out,
    qr, kr, vr, kd, vd, fd, qg, held, top, full, ob, att, wr, lhs, total,
    sent, got, w_sent, w_got, own,
):
    devices, _, width = qr.shape
    parts = wr.shape[0] // w.shape[0]
    me = lax.axis_index("seq")
    dp = lax.axis_index("dp")
    barrier = pltpu.get_barrier_semaphore()

    def hello(axis, size, at):
        def one(i):
            pl.semaphore_signal(
                barrier, 1, device_id={axis: lax.rem(at + i, size)}, device_id_type=MESH
            )

        loop(1, size, one)

    hello("seq", devices, me)
    hello("dp", parts, dp)
    pl.semaphore_wait(barrier, devices - 1 + parts - 1)

    def remote(t, i, src, dst, to, from_):
        return pltpu.make_async_remote_copy(
            src_ref=src,
            dst_ref=dst,
            send_sem=sent.at[t, i],
            recv_sem=got.at[t, from_],
            device_id={"seq": to},
            device_id_type=MESH,
        )

    pairs = [(q, qr), (k, kr), (v, vr)]

    def send(t, i):
        to = target(me, i)
        return remote(t, i, pairs[t][0].at[to], pairs[t][1].at[me], to, me)

    def arrive(t, i):
        s = source(me, i)
        remote(t, i, pairs[t][0].at[s], pairs[t][1].at[s], s, s).wait_recv()

    def send_w(i, at):
        to = lax.rem(dp + i, parts)
        return pltpu.make_async_remote_copy(
            src_ref=w,
            dst_ref=wr.at[pl.ds(at * w.shape[0], w.shape[0])],
            send_sem=w_sent.at[i],
            recv_sem=w_got.at[i],
            device_id={"dp": to},
            device_id_type=MESH,
        )

    copies = [pltpu.make_async_copy(a.at[me], b.at[me], own.at[t]) for t, (a, b) in enumerate(pairs)]
    copies.append(
        pltpu.make_async_copy(w, wr.at[pl.ds(dp * w.shape[0], w.shape[0])], own.at[3])
    )
    for t in range(3):
        loop(0, devices - 1, lambda i: send(t, i).start())
        copies[t].start()
        if t == 0:
            loop(1, parts, lambda i: send_w(i, dp).start())
            copies[3].start()

    qg[...] = jnp.zeros(qg.shape, qg.dtype)
    top[...] = jnp.full(top.shape, -jnp.inf, jnp.float32)
    full[...] = jnp.zeros(full.shape, jnp.float32)

    def take(t, f):
        copies[t].wait()

        def one(i):
            @pl.when(i < devices - 1)
            def _():
                arrive(t, i)

            f(source(me, i))

        loop(0, devices, one)

    take(0, lambda s: take_query(s, qr.at[s], qg, glob))
    take(1, lambda s: take_key(s, kr.at[s], kd, qg, held, top))
    take(2, lambda s: take_value(s, vr.at[s], vd, held, top, full))
    finish_full(full, fd)

    def send_o(i):
        to = target(me, i)
        return remote(3, i, ob.at[i], att.at[me], to, me)

    def project(g, last):
        rows = []
        heads = [source(me, g * GROUP + j) for j in range(GROUP)]
        for j in range(GROUP):
            s = heads[j]
            if not (last and j == GROUP - 1):
                remote(3, g * GROUP + j, ob.at[j], att.at[s], s, s).wait_recv()
            rows.append(att[s])
        lhs[...] = jnp.concatenate(rows, axis=0).T

        def tile(n):
            cols = pl.ds(pl.multiple_of(n * QUAD, QUAD), QUAD)
            part = dot(lhs[...], jnp.concatenate([wr[h, :, cols] for h in heads], axis=0))
            if last:
                out[:, cols] = (total[:, cols] + part).astype(jnp.bfloat16)
            else:
                total[:, cols] += part

        loop(0, out.shape[1] // QUAD, tile)

    total[...] = jnp.zeros(total.shape, jnp.float32)
    copies[3].wait()
    loop(1, parts, lambda i: send_w(i, lax.rem(dp + parts - i, parts)).wait_recv())

    def group(g):
        def one(j):
            i = g * GROUP + j
            d = target(me, i)
            for h in range(width // QUAD):
                cols = slice(h * QUAD, (h + 1) * QUAD)
                ob[i, :, cols] = attend_quad(
                    d * (width // QUAD) + h, qr[d, :, cols], kd, vd, fd, index, bias, glob
                )

            @pl.when(i > 0)
            def _():
                send_o(i - 1).start()

        loop(0, GROUP, one)

        @pl.when(g > 0)
        def _():
            project(g - 1, False)

    groups = devices // GROUP
    loop(0, groups, group)
    att[me] = ob[devices - 1]
    project(groups - 1, True)

    for t in range(3):
        loop(0, devices - 1, lambda i: send(t, i).wait_send())
    loop(0, devices - 1, lambda i: send_o(i).wait_send())
    loop(1, parts, lambda i: send_w(i, dp).wait_send())


def layer(index, glob, bias, q, k, v, w, parts):
    devices, _, width = q.shape
    blocks = devices * width // BLK
    columns = w.shape[2]
    bf = jnp.bfloat16
    dma = pltpu.SemaphoreType.DMA
    return pl.pallas_call(
        layer_kernel,
        out_shape=jax.ShapeDtypeStruct((width, columns), bf),
        in_specs=[SM, SM, VM, HB, HB, HB, HB],
        out_specs=VM,
        scratch_shapes=[
            pltpu.VMEM((devices, HD, width), bf),
            pltpu.VMEM((devices, HD, width), bf),
            pltpu.VMEM((devices, HD, width), bf),
            pltpu.VMEM((blocks, BLK, LANES), bf),
            pltpu.VMEM((blocks, HD, LANES), bf),
            pltpu.VMEM((2, HD, LANES), bf),
            pltpu.VMEM((HD, LANES), bf),
            pltpu.VMEM((devices, width // 2, 2 * LANES), jnp.float32),
            pltpu.VMEM((8, 2 * LANES), jnp.float32),
            pltpu.VMEM((2 * HD + 16, 2 * LANES), jnp.float32),
            pltpu.VMEM((devices, HD, width), bf),
            pltpu.VMEM((devices, HD, width), bf),
            pltpu.VMEM((w.shape[0] * parts, HD, columns), bf),
            pltpu.VMEM((width, GROUP * HD), bf),
            pltpu.VMEM((width, columns), jnp.float32),
            dma((4, devices)),
            dma((4, devices)),
            dma((parts,)),
            dma((parts,)),
            dma((4,)),
        ],
        compiler_params=pltpu.CompilerParams(
            collective_id=0, has_side_effects=True, vmem_limit_bytes=60 << 20
        ),
    )(index, glob, bias, q, k, v, w)


def local(queries, keys, values, random_blocks, global_blocks, out_weight):
    glob = global_blocks[0]
    width = queries.shape[2]
    index, bias = tables(glob, random_blocks[0, 0])
    q, k, v = (x[0].reshape(-1, HD, width) for x in (queries, keys, values))
    w = out_weight.reshape(-1, HD, out_weight.shape[1])
    parts = lax.axis_size("dp")
    return layer(index, glob, bias, q, k, v, w, parts)[None]


def solution(mesh):
    in_specs = (
        P("dp", None, "seq"),
        P("dp", None, "seq"),
        P("dp", None, "seq"),
        P("dp", "seq", None, None),
        P("dp", None),
        P("dp", None),
    )
    out_specs = P("dp", "seq", None)
    return jax.shard_map(local, mesh=mesh, in_specs=in_specs, out_specs=out_specs, check_vma=False)
```

```python
import functools

import jax
import jax.numpy as jnp
from jax import lax
from jax.experimental import pallas as pl
from jax.experimental.pallas import tpu as pltpu
from jax.sharding import PartitionSpec as P

HD = 64
BLK = 64
LANES = 128
CAND = 8
QUAD = 4 * BLK
SCALE = HD ** (-0.5) * 1.4426950408889634
MESH = pl.DeviceIdType.MESH


def dot(a, b):
    return lax.dot_general(a, b, (((1,), (0,)), ((), ())), preferred_element_type=jnp.float32)


def lane(shape):
    return lax.broadcasted_iota(jnp.int32, shape, len(shape) - 1)


def low_half(rows):
    return lane((rows, LANES)) < BLK


def swap(x):
    return jnp.concatenate([x[:, BLK:], x[:, :BLK]], axis=1)


def candidates(block, blocks, rand, glob):
    return [
        jnp.maximum(block - 1, 0),
        block,
        jnp.minimum(block + 1, blocks - 1),
        glob[0, 0],
        glob[0, 1],
    ] + [rand[r, 0, block] for r in range(CAND - 5)]


def mark_quad(quad, blocks, bias, rand, glob):
    at = lane((1, QUAD)) // BLK
    block = quad * 4 + at
    cand = [jnp.maximum(block - 1, 0), block, jnp.minimum(block + 1, blocks - 1)]
    cand += [jnp.full((1, QUAD), glob[0, g], jnp.int32) for g in range(2)]
    for r in range(CAND - 5):
        x = [rand[r, 0, quad * 4 + a] for a in range(4)]
        cand.append(
            jnp.where(at == 0, x[0], jnp.where(at == 1, x[1], jnp.where(at == 2, x[2], x[3])))
        )
    marks = [
        jnp.where(block == 0, -jnp.inf, 0.0),
        jnp.zeros((1, QUAD), jnp.float32),
        jnp.where(block == blocks - 1, -jnp.inf, 0.0),
    ]
    for c in range(3, CAND):
        seen = cand[c] == cand[0]
        for e in range(1, c):
            seen = seen | (cand[c] == cand[e])
        marks.append(jnp.where(seen, -jnp.inf, 0.0))
    for c in range(CAND):
        bias[quad, c : c + 1, :] = marks[c].astype(jnp.float32)


def take_query(s, q, qg, glob):
    at = lane((HD, LANES))
    want = jnp.where(at < BLK, glob[0, 0], glob[0, 1])
    kept = qg[...]
    for i in range(q.shape[1] // LANES):
        x = q[:, i * LANES : (i + 1) * LANES]
        first = s * (q.shape[1] // BLK) + 2 * i
        here = first + jnp.where(at < BLK, 0, 1)
        there = first + jnp.where(at < BLK, 1, 0)
        kept = jnp.where(here == want, x, jnp.where(there == want, swap(x), kept))
    qg[...] = kept


def take_key(s, k, kd, qg, held, top):
    per = k.shape[1] // BLK
    tokens = jnp.concatenate([k[...], k[...]], axis=0).T
    for i in range(per):
        kd[s * per + i] = tokens[i * BLK : (i + 1) * BLK, :]
    half = k.shape[1] // 2
    pairs = jnp.where(low_half(half), tokens[:half, :], tokens[half:, :])
    g = qg[...]
    zero = jnp.zeros_like(g)
    weights = jnp.concatenate(
        [jnp.concatenate([g, zero], axis=1), jnp.concatenate([zero, g], axis=1)], axis=0
    )
    scores = dot(pairs, weights) * SCALE
    held[s] = scores
    best = top[...]
    for r in range(half // 8):
        best = jnp.maximum(best, scores[r * 8 : (r + 1) * 8, :])
    top[...] = best


def top_of(top):
    best = jnp.max(top[...], axis=0, keepdims=True)
    best = jnp.maximum(best[:, :LANES], best[:, LANES:])
    return jnp.concatenate([best, best], axis=1)


def take_value(s, v, vd, held, top, full):
    per = v.shape[1] // BLK
    low = low_half(HD)
    for i in range(per // 2):
        x = v[:, i * LANES : (i + 1) * LANES]
        y = swap(x)
        vd[s * per + 2 * i] = jnp.where(low, x, y)
        vd[s * per + 2 * i + 1] = jnp.where(low, y, x)
    half = v.shape[1] // 2
    probs = jnp.exp2(held[s] - top_of(top)).astype(jnp.bfloat16)
    ones = jnp.ones((16, half), jnp.bfloat16)
    lhs = jnp.concatenate([v[:, :half], v[:, half:], ones], axis=0)
    full[...] += dot(lhs, probs)


def finish_full(full, fd):
    num = full[:HD, :LANES] + full[HD : 2 * HD, LANES:]
    row = full[2 * HD : 2 * HD + 1, :]
    out = (num / (row[:, :LANES] + row[:, LANES:])).astype(jnp.bfloat16)
    low = low_half(HD)
    other = swap(out)
    fd[0] = jnp.where(low, out, other)
    fd[1] = jnp.where(low, other, out)


def attend_quad(quad, qq, kd, vd, fd, rand, bias, glob):
    low = low_half(BLK)
    at = lane((HD, QUAD)) // BLK
    zero = jnp.zeros_like(qq)
    weights = jnp.concatenate([jnp.where(at == a, qq, zero) for a in range(4)], axis=0)
    picks = [candidates(quad * 4 + a, kd.shape[0], rand, glob) for a in range(4)]
    keys = []
    for c in range(CAND):
        k = [kd[picks[a][c]] for a in range(4)]
        keys.append(
            jnp.concatenate([jnp.where(low, k[0], k[1]), jnp.where(low, k[2], k[3])], axis=1)
        )
    scores = dot(jnp.concatenate(keys, axis=0), weights) * SCALE
    marks = bias[quad]
    scores = jnp.concatenate(
        [scores[c * BLK : (c + 1) * BLK, :] + marks[c : c + 1, :] for c in range(CAND)], axis=0
    )
    top = jnp.max(scores, axis=0, keepdims=True)
    probs = jnp.exp2(scores - top).astype(jnp.bfloat16)
    vals = []
    for a in range(4):
        v = [vd[picks[a][c]] for c in range(CAND)]
        vals.append(
            jnp.concatenate(
                [jnp.where(low, v[2 * g], v[2 * g + 1]) for g in range(CAND // 2)], axis=1
            )
        )
    vals.append(jnp.ones((16, CAND * BLK), jnp.bfloat16))
    got = dot(jnp.concatenate(vals, axis=0), probs)
    num = jnp.concatenate(
        [
            jnp.where(low, got[0:64, :LANES], got[64:128, :LANES]),
            jnp.where(low, got[128:192, LANES:], got[192:256, LANES:]),
        ],
        axis=1,
    )
    out = (num / got[256:257, :]).astype(jnp.bfloat16)
    here = quad * 4 + at
    for g in range(2):
        f = fd[g]
        out = jnp.where(here == glob[0, g], jnp.concatenate([f, f], axis=1), out)
    return out


VM = pl.BlockSpec(memory_space=pltpu.VMEM)
SM = pl.BlockSpec(memory_space=pltpu.SMEM)
HB = pl.BlockSpec(memory_space=pl.ANY)

NY = 4
NZ = 8
GROUP = 4


def offset(i, near):
    a = i // NY
    step = ((a + 1) // 2) * (1 - 2 * lax.rem(a, 2))
    far = NZ // 2 + step
    b = lax.rem(a + 1, NZ)
    close = NZ + ((b + 1) // 2) * (2 * lax.rem(b, 2) - 1)
    return lax.rem(i + 1, NY), (lax.rem(close, NZ) if near else far)


def target(me, i, near):
    dy, dz = offset(i, near)
    return lax.rem(me // NZ + dy, NY) * NZ + lax.rem(lax.rem(me, NZ) + dz, NZ)


def source(me, i, near):
    dy, dz = offset(i, near)
    return lax.rem(me // NZ + NY - dy, NY) * NZ + lax.rem(lax.rem(me, NZ) + NZ - dz, NZ)


def loop(first, last, f):
    def body(i, c):
        f(i)
        return c

    lax.fori_loop(first, last, body, 0)


def layer_kernel(
    glob, rand_hbm, q, k, v, w, out,
    rand, bias, qr, kr, vr, kd, vd, fd, qg, held, top, full, ob, att, wr, lhs, total,
    sent, got, w_sent, w_got, own,
):
    devices, _, width = qr.shape
    parts = wr.shape[0] // w.shape[0]
    me = lax.axis_index("seq")
    dp = lax.axis_index("dp")
    barrier = pltpu.get_barrier_semaphore()

    def hello(axis, size, at):
        def one(i):
            pl.semaphore_signal(
                barrier, 1, device_id={axis: lax.rem(at + i, size)}, device_id_type=MESH
            )

        loop(1, size, one)

    hello("seq", devices, me)
    hello("dp", parts, dp)
    pl.semaphore_wait(barrier, devices - 1 + parts - 1)

    def remote(t, i, src, dst, to, from_):
        return pltpu.make_async_remote_copy(
            src_ref=src,
            dst_ref=dst,
            send_sem=sent.at[t, i],
            recv_sem=got.at[t, from_],
            device_id={"seq": to},
            device_id_type=MESH,
        )

    pairs = [(q, qr), (k, kr), (v, vr)]

    def send(t, i):
        to = target(me, i, True)
        return remote(t, i, pairs[t][0].at[to], pairs[t][1].at[me], to, me)

    def arrive(t, i):
        s = source(me, i, True)
        remote(t, i, pairs[t][0].at[s], pairs[t][1].at[s], s, s).wait_recv()

    def send_w(i, at):
        to = lax.rem(dp + i, parts)
        return pltpu.make_async_remote_copy(
            src_ref=w,
            dst_ref=wr.at[pl.ds(at * w.shape[0], w.shape[0])],
            send_sem=w_sent.at[i],
            recv_sem=w_got.at[i],
            device_id={"dp": to},
            device_id_type=MESH,
        )

    copies = [pltpu.make_async_copy(a.at[me], b.at[me], own.at[t]) for t, (a, b) in enumerate(pairs)]
    table = pltpu.make_async_copy(rand_hbm, rand, own.at[4])
    table.start()
    copies.append(
        pltpu.make_async_copy(w, wr.at[pl.ds(dp * w.shape[0], w.shape[0])], own.at[3])
    )
    for t in range(3):
        loop(0, devices - 1, lambda i: send(t, i).start())
        copies[t].start()
        if t == 0:
            loop(1, parts, lambda i: send_w(i, dp).start())
            copies[3].start()

    qg[...] = jnp.zeros(qg.shape, qg.dtype)
    top[...] = jnp.full(top.shape, -jnp.inf, jnp.float32)
    full[...] = jnp.zeros(full.shape, jnp.float32)

    def take(t, f):
        copies[t].wait()

        def one(i):
            @pl.when(i < devices - 1)
            def _():
                arrive(t, i)

            f(source(me, i, True))

        loop(0, devices, one)

    table.wait()

    def first(s):
        for h in range(width // QUAD):
            mark_quad(s * (width // QUAD) + h, kd.shape[0], bias, rand, glob)
        take_query(s, qr.at[s], qg, glob)

    take(0, first)
    take(1, lambda s: take_key(s, kr.at[s], kd, qg, held, top))
    take(2, lambda s: take_value(s, vr.at[s], vd, held, top, full))
    finish_full(full, fd)

    def send_o(i):
        to = target(me, i, False)
        return remote(3, i, ob.at[i], att.at[me], to, me)

    def chunk(i):
        d = target(me, i, False)
        for h in range(width // QUAD):
            cols = slice(h * QUAD, (h + 1) * QUAD)
            ob[i, :, cols] = attend_quad(
                d * (width // QUAD) + h, qr[d, :, cols], kd, vd, fd, rand, bias, glob
            )

        @pl.when(i > 0)
        def _():
            send_o(i - 1).start()

    loop(0, devices, chunk)
    att[me] = ob[devices - 1]
    copies[3].wait()
    loop(1, parts, lambda i: send_w(i, lax.rem(dp + parts - i, parts)).wait_recv())

    def project(g, step):
        heads = [source(me, g * GROUP + j, False) for j in range(GROUP)]
        for j in range(GROUP):
            if not (step == 2 and j == GROUP - 1):
                s = heads[j]
                remote(3, g * GROUP + j, ob.at[j], att.at[s], s, s).wait_recv()
        lhs[...] = jnp.concatenate([att[s] for s in heads], axis=0).T

        def tile(n):
            cols = pl.ds(pl.multiple_of(n * QUAD, QUAD), QUAD)
            part = dot(lhs[...], jnp.concatenate([wr[h, :, cols] for h in heads], axis=0))
            if step == 0:
                total[:, cols] = part
            elif step == 1:
                total[:, cols] += part
            else:
                out[:, cols] = (total[:, cols] + part).astype(jnp.bfloat16)

        loop(0, out.shape[1] // QUAD, tile)

    groups = devices // GROUP
    project(0, 0)
    loop(1, groups - 1, lambda g: project(g, 1))
    project(groups - 1, 2)

    for t in range(3):
        loop(0, devices - 1, lambda i: send(t, i).wait_send())
    loop(0, devices - 1, lambda i: send_o(i).wait_send())
    loop(1, parts, lambda i: send_w(i, dp).wait_send())


def layer(glob, rand, q, k, v, w, parts):
    devices, _, width = q.shape
    blocks = devices * width // BLK
    columns = w.shape[2]
    bf = jnp.bfloat16
    dma = pltpu.SemaphoreType.DMA
    return pl.pallas_call(
        layer_kernel,
        out_shape=jax.ShapeDtypeStruct((width, columns), bf),
        in_specs=[SM, HB, HB, HB, HB, HB],
        out_specs=VM,
        scratch_shapes=[
            pltpu.SMEM(rand.shape, jnp.int32),
            pltpu.VMEM((blocks // 4, CAND, QUAD), jnp.float32),
            pltpu.VMEM((devices, HD, width), bf),
            pltpu.VMEM((devices, HD, width), bf),
            pltpu.VMEM((devices, HD, width), bf),
            pltpu.VMEM((blocks, BLK, LANES), bf),
            pltpu.VMEM((blocks, HD, LANES), bf),
            pltpu.VMEM((2, HD, LANES), bf),
            pltpu.VMEM((HD, LANES), bf),
            pltpu.VMEM((devices, width // 2, 2 * LANES), jnp.float32),
            pltpu.VMEM((8, 2 * LANES), jnp.float32),
            pltpu.VMEM((2 * HD + 16, 2 * LANES), jnp.float32),
            pltpu.VMEM((devices, HD, width), bf),
            pltpu.VMEM((devices, HD, width), bf),
            pltpu.VMEM((w.shape[0] * parts, HD, columns), bf),
            pltpu.VMEM((width, GROUP * HD), bf),
            pltpu.VMEM((width, columns), jnp.float32),
            dma((4, devices)),
            dma((4, devices)),
            dma((parts,)),
            dma((parts,)),
            dma((5,)),
        ],
        compiler_params=pltpu.CompilerParams(
            collective_id=0, has_side_effects=True, vmem_limit_bytes=60 << 20
        ),
    )(glob, rand, q, k, v, w)


def local(queries, keys, values, random_blocks, global_blocks, out_weight):
    width = queries.shape[2]
    q, k, v = (x[0].reshape(-1, HD, width) for x in (queries, keys, values))
    w = out_weight.reshape(-1, HD, out_weight.shape[1])
    parts = lax.axis_size("dp")
    return layer(global_blocks, random_blocks.transpose(0, 3, 1, 2)[0], q, k, v, w, parts)[None]


def solution(mesh):
    in_specs = (
        P("dp", None, "seq"),
        P("dp", None, "seq"),
        P("dp", None, "seq"),
        P("dp", "seq", None, None),
        P("dp", None),
        P("dp", None),
    )
    out_specs = P("dp", "seq", None)
    return jax.shard_map(local, mesh=mesh, in_specs=in_specs, out_specs=out_specs, check_vma=False)
```

```python
import functools

import jax
import jax.numpy as jnp
from jax import lax
from jax.experimental import pallas as pl
from jax.experimental.pallas import tpu as pltpu
from jax.sharding import PartitionSpec as P

HD = 64
BLK = 64
LANES = 128
CAND = 8
QUAD = 4 * BLK
SCALE = HD ** (-0.5) * 1.4426950408889634
MESH = pl.DeviceIdType.MESH


def dot(a, b):
    return lax.dot_general(a, b, (((1,), (0,)), ((), ())), preferred_element_type=jnp.float32)


def lane(shape):
    return lax.broadcasted_iota(jnp.int32, shape, len(shape) - 1)


def low_half(rows):
    return lane((rows, LANES)) < BLK


def swap(x):
    return jnp.concatenate([x[:, BLK:], x[:, :BLK]], axis=1)


def candidates(block, blocks, rand, glob):
    return [
        jnp.maximum(block - 1, 0),
        block,
        jnp.minimum(block + 1, blocks - 1),
        glob[0, 0],
        glob[0, 1],
    ] + [rand[r, 0, block] for r in range(CAND - 5)]


def mark_quad(quad, blocks, bias, rand, glob):
    at = lane((1, QUAD)) // BLK
    block = quad * 4 + at
    cand = [jnp.maximum(block - 1, 0), block, jnp.minimum(block + 1, blocks - 1)]
    cand += [jnp.full((1, QUAD), glob[0, g], jnp.int32) for g in range(2)]
    for r in range(CAND - 5):
        x = [rand[r, 0, quad * 4 + a] for a in range(4)]
        cand.append(
            jnp.where(at == 0, x[0], jnp.where(at == 1, x[1], jnp.where(at == 2, x[2], x[3])))
        )
    marks = [
        jnp.where(block == 0, -jnp.inf, 0.0),
        jnp.zeros((1, QUAD), jnp.float32),
        jnp.where(block == blocks - 1, -jnp.inf, 0.0),
    ]
    for c in range(3, CAND):
        seen = cand[c] == cand[0]
        for e in range(1, c):
            seen = seen | (cand[c] == cand[e])
        marks.append(jnp.where(seen, -jnp.inf, 0.0))
    for c in range(CAND):
        bias[quad, c : c + 1, :] = marks[c].astype(jnp.float32)


def take_query(s, q, qg, glob):
    at = lane((HD, LANES))
    want = jnp.where(at < BLK, glob[0, 0], glob[0, 1])
    kept = qg[...]
    for i in range(q.shape[1] // LANES):
        x = q[:, i * LANES : (i + 1) * LANES]
        first = s * (q.shape[1] // BLK) + 2 * i
        here = first + jnp.where(at < BLK, 0, 1)
        there = first + jnp.where(at < BLK, 1, 0)
        kept = jnp.where(here == want, x, jnp.where(there == want, swap(x), kept))
    qg[...] = kept


def take_key(s, k, kd, qg, held, top):
    per = k.shape[1] // BLK
    tokens = jnp.concatenate([k[...], k[...]], axis=0).T
    for i in range(per):
        kd[s * per + i] = tokens[i * BLK : (i + 1) * BLK, :]
    half = k.shape[1] // 2
    pairs = jnp.where(low_half(half), tokens[:half, :], tokens[half:, :])
    g = qg[...]
    zero = jnp.zeros_like(g)
    weights = jnp.concatenate(
        [jnp.concatenate([g, zero], axis=1), jnp.concatenate([zero, g], axis=1)], axis=0
    )
    scores = dot(pairs, weights) * SCALE
    held[s] = scores
    best = top[...]
    for r in range(half // 8):
        best = jnp.maximum(best, scores[r * 8 : (r + 1) * 8, :])
    top[...] = best


def top_of(top):
    best = jnp.max(top[...], axis=0, keepdims=True)
    best = jnp.maximum(best[:, :LANES], best[:, LANES:])
    return jnp.concatenate([best, best], axis=1)


def weigh(s, held, best, probs):
    probs[s] = jnp.exp2(held[s] - best).astype(jnp.bfloat16)


def take_value(s, v, vd, probs, full):
    per = v.shape[1] // BLK
    low = low_half(HD)
    for i in range(per // 2):
        x = v[:, i * LANES : (i + 1) * LANES]
        y = swap(x)
        vd[s * per + 2 * i] = jnp.where(low, x, y)
        vd[s * per + 2 * i + 1] = jnp.where(low, y, x)
    half = v.shape[1] // 2
    ones = jnp.ones((16, half), jnp.bfloat16)
    lhs = jnp.concatenate([v[:, :half], v[:, half:], ones], axis=0)
    full[...] += dot(lhs, probs[s])


def finish_full(full, fd):
    num = full[:HD, :LANES] + full[HD : 2 * HD, LANES:]
    row = full[2 * HD : 2 * HD + 1, :]
    out = (num / (row[:, :LANES] + row[:, LANES:])).astype(jnp.bfloat16)
    low = low_half(HD)
    other = swap(out)
    fd[0] = jnp.where(low, out, other)
    fd[1] = jnp.where(low, other, out)


def attend_quad(quad, qq, kd, vd, fd, rand, bias, glob):
    low = low_half(BLK)
    at = lane((HD, QUAD)) // BLK
    zero = jnp.zeros_like(qq)
    weights = jnp.concatenate([jnp.where(at == a, qq, zero) for a in range(4)], axis=0)
    picks = [candidates(quad * 4 + a, kd.shape[0], rand, glob) for a in range(4)]
    keys = []
    for c in range(CAND):
        k = [kd[picks[a][c]] for a in range(4)]
        keys.append(
            jnp.concatenate([jnp.where(low, k[0], k[1]), jnp.where(low, k[2], k[3])], axis=1)
        )
    scores = dot(jnp.concatenate(keys, axis=0), weights) * SCALE
    marks = bias[quad]
    scores = jnp.concatenate(
        [scores[c * BLK : (c + 1) * BLK, :] + marks[c : c + 1, :] for c in range(CAND)], axis=0
    )
    top = jnp.max(scores, axis=0, keepdims=True)
    probs = jnp.exp2(scores - top).astype(jnp.bfloat16)
    vals = []
    for a in range(4):
        v = [vd[picks[a][c]] for c in range(CAND)]
        vals.append(
            jnp.concatenate(
                [jnp.where(low, v[2 * g], v[2 * g + 1]) for g in range(CAND // 2)], axis=1
            )
        )
    vals.append(jnp.ones((16, CAND * BLK), jnp.bfloat16))
    got = dot(jnp.concatenate(vals, axis=0), probs)
    num = jnp.concatenate(
        [
            jnp.where(low, got[0:64, :LANES], got[64:128, :LANES]),
            jnp.where(low, got[128:192, LANES:], got[192:256, LANES:]),
        ],
        axis=1,
    )
    out = (num / got[256:257, :]).astype(jnp.bfloat16)
    here = quad * 4 + at
    for g in range(2):
        f = fd[g]
        out = jnp.where(here == glob[0, g], jnp.concatenate([f, f], axis=1), out)
    return out


VM = pl.BlockSpec(memory_space=pltpu.VMEM)
SM = pl.BlockSpec(memory_space=pltpu.SMEM)
HB = pl.BlockSpec(memory_space=pltpu.HBM)

NY = 4
NZ = 8
GROUP = 4


def offset(i, near):
    a = i // NY
    step = ((a + 1) // 2) * (1 - 2 * lax.rem(a, 2))
    far = NZ // 2 + step
    b = lax.rem(a + 1, NZ)
    close = NZ + ((b + 1) // 2) * (2 * lax.rem(b, 2) - 1)
    return lax.rem(i + 1, NY), (lax.rem(close, NZ) if near else far)


def target(me, i, near):
    dy, dz = offset(i, near)
    return lax.rem(me // NZ + dy, NY) * NZ + lax.rem(lax.rem(me, NZ) + dz, NZ)


def source(me, i, near):
    dy, dz = offset(i, near)
    return lax.rem(me // NZ + NY - dy, NY) * NZ + lax.rem(lax.rem(me, NZ) + NZ - dz, NZ)


def loop(first, last, f):
    def body(i, c):
        f(i)
        return c

    lax.fori_loop(first, last, body, 0)


def layer_kernel(
    glob, rand_hbm, q, k, v, w, out,
    rand, bias, qr, kr, vr, kd, vd, fd, qg, held, probs, top, full, ob, att, wr, lhs, total,
    sent, got, w_sent, w_got, own,
):
    devices, _, width = qr.shape
    parts = wr.shape[0] // w.shape[0]
    me = lax.axis_index("seq")
    dp = lax.axis_index("dp")
    barrier = pltpu.get_barrier_semaphore()

    def hello(axis, size, at):
        def one(i):
            pl.semaphore_signal(
                barrier, 1, device_id={axis: lax.rem(at + i, size)}, device_id_type=MESH
            )

        loop(1, size, one)

    hello("seq", devices, me)
    hello("dp", parts, dp)
    pl.semaphore_wait(barrier, devices - 1 + parts - 1)

    def remote(t, i, src, dst, to, from_):
        return pltpu.make_async_remote_copy(
            src_ref=src,
            dst_ref=dst,
            send_sem=sent.at[t, i],
            recv_sem=got.at[t, from_],
            device_id={"seq": to},
            device_id_type=MESH,
        )

    pairs = [(q, qr), (k, kr), (v, vr)]

    def send(t, i):
        to = target(me, i, True)
        return remote(t, i, pairs[t][0].at[to], pairs[t][1].at[me], to, me)

    def arrive(t, i):
        s = source(me, i, True)
        remote(t, i, pairs[t][0].at[s], pairs[t][1].at[s], s, s).wait_recv()

    def send_w(i, at):
        to = lax.rem(dp + i, parts)
        return pltpu.make_async_remote_copy(
            src_ref=w,
            dst_ref=wr.at[pl.ds(at * w.shape[0], w.shape[0])],
            send_sem=w_sent.at[i],
            recv_sem=w_got.at[i],
            device_id={"dp": to},
            device_id_type=MESH,
        )

    copies = [pltpu.make_async_copy(a.at[me], b.at[me], own.at[t]) for t, (a, b) in enumerate(pairs)]
    table = pltpu.make_async_copy(rand_hbm, rand, own.at[4])
    table.start()
    copies.append(
        pltpu.make_async_copy(w, wr.at[pl.ds(dp * w.shape[0], w.shape[0])], own.at[3])
    )
    for t in range(3):
        loop(0, devices - 1, lambda i: send(t, i).start())
        copies[t].start()
        if t == 0:
            loop(1, parts, lambda i: send_w(i, dp).start())
            copies[3].start()

    qg[...] = jnp.zeros(qg.shape, qg.dtype)
    top[...] = jnp.full(top.shape, -jnp.inf, jnp.float32)
    full[...] = jnp.zeros(full.shape, jnp.float32)

    def take(t, f):
        copies[t].wait()

        def one(i):
            @pl.when(i < devices - 1)
            def _():
                arrive(t, i)

            f(source(me, i, True))

        loop(0, devices, one)

    table.wait()

    def first(s):
        for h in range(width // QUAD):
            mark_quad(s * (width // QUAD) + h, kd.shape[0], bias, rand, glob)
        take_query(s, qr.at[s], qg, glob)

    take(0, first)
    take(1, lambda s: take_key(s, kr.at[s], kd, qg, held, top))
    best = top_of(top)
    loop(0, devices, lambda s: weigh(s, held, best, probs))
    take(2, lambda s: take_value(s, vr.at[s], vd, probs, full))
    finish_full(full, fd)

    def send_o(i):
        to = target(me, i, False)
        return remote(3, i, ob.at[i], att.at[me], to, me)

    def chunk(i):
        d = target(me, i, False)
        for h in range(width // QUAD):
            cols = slice(h * QUAD, (h + 1) * QUAD)
            ob[i, :, cols] = attend_quad(
                d * (width // QUAD) + h, qr[d, :, cols], kd, vd, fd, rand, bias, glob
            )

        @pl.when(i > 0)
        def _():
            send_o(i - 1).start()

    loop(0, devices, chunk)
    att[me] = ob[devices - 1]
    for t in range(3):
        loop(0, devices - 1, lambda i: send(t, i).wait_send())
    copies[3].wait()
    loop(1, parts, lambda i: send_w(i, lax.rem(dp + parts - i, parts)).wait_recv())

    def project(g, step):
        heads = [source(me, g * GROUP + j, False) for j in range(GROUP)]
        for j in range(GROUP):
            if not (step == 2 and j == GROUP - 1):
                s = heads[j]
                remote(3, g * GROUP + j, ob.at[j], att.at[s], s, s).wait_recv()
        lhs[...] = jnp.concatenate([att[s] for s in heads], axis=0).T

        def tile(n):
            cols = pl.ds(pl.multiple_of(n * QUAD, QUAD), QUAD)
            part = dot(lhs[...], jnp.concatenate([wr[h, :, cols] for h in heads], axis=0))
            if step == 0:
                total[:, cols] = part
            elif step == 1:
                total[:, cols] += part
            else:
                out[:, cols] = (total[:, cols] + part).astype(jnp.bfloat16)

        loop(0, out.shape[1] // QUAD, tile)

    groups = devices // GROUP
    project(0, 0)
    loop(1, groups - 1, lambda g: project(g, 1))
    project(groups - 1, 2)

    loop(0, devices - 1, lambda i: send_o(i).wait_send())
    loop(1, parts, lambda i: send_w(i, dp).wait_send())


def layer(glob, rand, q, k, v, w, parts):
    devices, _, width = q.shape
    blocks = devices * width // BLK
    columns = w.shape[2]
    bf = jnp.bfloat16
    dma = pltpu.SemaphoreType.DMA
    return pl.pallas_call(
        layer_kernel,
        out_shape=pltpu.VMEM((width, columns), bf),
        in_specs=[SM, HB, HB, HB, HB, HB],
        out_specs=VM,
        scratch_shapes=[
            pltpu.SMEM(rand.shape, jnp.int32),
            pltpu.VMEM((blocks // 4, CAND, QUAD), jnp.float32),
            pltpu.VMEM((devices, HD, width), bf),
            pltpu.VMEM((devices, HD, width), bf),
            pltpu.VMEM((devices, HD, width), bf),
            pltpu.VMEM((blocks, BLK, LANES), bf),
            pltpu.VMEM((blocks, HD, LANES), bf),
            pltpu.VMEM((2, HD, LANES), bf),
            pltpu.VMEM((HD, LANES), bf),
            pltpu.VMEM((devices, width // 2, 2 * LANES), jnp.float32),
            pltpu.VMEM((devices, width // 2, 2 * LANES), bf),
            pltpu.VMEM((8, 2 * LANES), jnp.float32),
            pltpu.VMEM((2 * HD + 16, 2 * LANES), jnp.float32),
            pltpu.VMEM((devices, HD, width), bf),
            pltpu.VMEM((devices, HD, width), bf),
            pltpu.VMEM((w.shape[0] * parts, HD, columns), bf),
            pltpu.VMEM((width, GROUP * HD), bf),
            pltpu.VMEM((width, columns), jnp.float32),
            dma((4, devices)),
            dma((4, devices)),
            dma((parts,)),
            dma((parts,)),
            dma((5,)),
        ],
        compiler_params=pltpu.CompilerParams(
            collective_id=0, has_side_effects=True, vmem_limit_bytes=54 << 20
        ),
    )(glob, rand, q, k, v, w)


def local(queries, keys, values, random_blocks, global_blocks, out_weight):
    width = queries.shape[2]
    q, k, v = (x[0].reshape(-1, HD, width) for x in (queries, keys, values))
    w = out_weight.reshape(-1, HD, out_weight.shape[1])
    parts = lax.axis_size("dp")
    return layer(global_blocks, random_blocks.transpose(0, 3, 1, 2)[0], q, k, v, w, parts)[None]


def solution(mesh):
    in_specs = (
        P("dp", None, "seq"),
        P("dp", None, "seq"),
        P("dp", None, "seq"),
        P("dp", "seq", None, None),
        P("dp", None),
        P("dp", None),
    )
    out_specs = P("dp", "seq", None)
    return jax.shard_map(local, mesh=mesh, in_specs=in_specs, out_specs=out_specs, check_vma=False)
```

```python
import functools

import jax
import jax.numpy as jnp
from jax import lax
from jax.experimental import pallas as pl
from jax.experimental.pallas import tpu as pltpu
from jax.sharding import PartitionSpec as P

HD = 64
BLK = 64
LANES = 128
CAND = 8
QUAD = 4 * BLK
SCALE = HD ** (-0.5) * 1.4426950408889634
MESH = pl.DeviceIdType.MESH


def dot(a, b):
    return lax.dot_general(a, b, (((1,), (0,)), ((), ())), preferred_element_type=jnp.float32)


def lane(shape):
    return lax.broadcasted_iota(jnp.int32, shape, len(shape) - 1)


def low_half(rows):
    return lane((rows, LANES)) < BLK


def swap(x):
    return jnp.concatenate([x[:, BLK:], x[:, :BLK]], axis=1)


def candidates(block, blocks, rand, glob):
    return [
        jnp.maximum(block - 1, 0),
        block,
        jnp.minimum(block + 1, blocks - 1),
        glob[0, 0],
        glob[0, 1],
    ] + [rand[r, 0, block] for r in range(CAND - 5)]


def mark_quad(quad, blocks, bias, rand, glob):
    at = lane((1, QUAD)) // BLK
    block = quad * 4 + at
    cand = [jnp.maximum(block - 1, 0), block, jnp.minimum(block + 1, blocks - 1)]
    cand += [jnp.full((1, QUAD), glob[0, g], jnp.int32) for g in range(2)]
    for r in range(CAND - 5):
        x = [rand[r, 0, quad * 4 + a] for a in range(4)]
        cand.append(
            jnp.where(at == 0, x[0], jnp.where(at == 1, x[1], jnp.where(at == 2, x[2], x[3])))
        )
    marks = [
        jnp.where(block == 0, -jnp.inf, 0.0),
        jnp.zeros((1, QUAD), jnp.float32),
        jnp.where(block == blocks - 1, -jnp.inf, 0.0),
    ]
    for c in range(3, CAND):
        seen = cand[c] == cand[0]
        for e in range(1, c):
            seen = seen | (cand[c] == cand[e])
        marks.append(jnp.where(seen, -jnp.inf, 0.0))
    for c in range(CAND):
        bias[quad, c : c + 1, :] = marks[c].astype(jnp.float32)


def take_query(s, q, qg, glob):
    at = lane((HD, LANES))
    want = jnp.where(at < BLK, glob[0, 0], glob[0, 1])
    kept = qg[...]
    for i in range(q.shape[1] // LANES):
        x = q[:, i * LANES : (i + 1) * LANES]
        first = s * (q.shape[1] // BLK) + 2 * i
        here = first + jnp.where(at < BLK, 0, 1)
        there = first + jnp.where(at < BLK, 1, 0)
        kept = jnp.where(here == want, x, jnp.where(there == want, swap(x), kept))
    qg[...] = kept


def take_key(s, k, kd, qg, held, top):
    per = k.shape[1] // BLK
    tokens = jnp.concatenate([k[...], k[...]], axis=0).T
    for i in range(per):
        kd[s * per + i] = tokens[i * BLK : (i + 1) * BLK, :]
    half = k.shape[1] // 2
    pairs = jnp.where(low_half(half), tokens[:half, :], tokens[half:, :])
    g = qg[...]
    zero = jnp.zeros_like(g)
    weights = jnp.concatenate(
        [jnp.concatenate([g, zero], axis=1), jnp.concatenate([zero, g], axis=1)], axis=0
    )
    scores = dot(pairs, weights) * SCALE
    held[s] = scores
    best = top[...]
    for r in range(half // 8):
        best = jnp.maximum(best, scores[r * 8 : (r + 1) * 8, :])
    top[...] = best


def top_of(top):
    best = jnp.max(top[...], axis=0, keepdims=True)
    best = jnp.maximum(best[:, :LANES], best[:, LANES:])
    return jnp.concatenate([best, best], axis=1)


def weigh(s, held, best, probs):
    probs[s] = jnp.exp2(held[s] - best).astype(jnp.bfloat16)


def take_value(s, v, vd, probs, full):
    per = v.shape[1] // BLK
    low = low_half(HD)
    for i in range(per // 2):
        x = v[:, i * LANES : (i + 1) * LANES]
        y = swap(x)
        vd[s * per + 2 * i] = jnp.where(low, x, y)
        vd[s * per + 2 * i + 1] = jnp.where(low, y, x)
    half = v.shape[1] // 2
    ones = jnp.ones((16, half), jnp.bfloat16)
    lhs = jnp.concatenate([v[:, :half], v[:, half:], ones], axis=0)
    full[...] += dot(lhs, probs[s])


def finish_full(full, fd):
    num = full[:HD, :LANES] + full[HD : 2 * HD, LANES:]
    row = full[2 * HD : 2 * HD + 1, :]
    out = (num / (row[:, :LANES] + row[:, LANES:])).astype(jnp.bfloat16)
    low = low_half(HD)
    other = swap(out)
    fd[0] = jnp.where(low, out, other)
    fd[1] = jnp.where(low, other, out)


def attend_quad(quad, qq, kd, vd, fd, rand, bias, glob):
    low = low_half(BLK)
    at = lane((HD, QUAD)) // BLK
    zero = jnp.zeros_like(qq)
    weights = jnp.concatenate([jnp.where(at == a, qq, zero) for a in range(4)], axis=0)
    picks = [candidates(quad * 4 + a, kd.shape[0], rand, glob) for a in range(4)]
    keys = []
    for c in range(CAND):
        k = [kd[picks[a][c]] for a in range(4)]
        keys.append(
            jnp.concatenate([jnp.where(low, k[0], k[1]), jnp.where(low, k[2], k[3])], axis=1)
        )
    scores = dot(jnp.concatenate(keys, axis=0), weights) * SCALE
    marks = bias[quad]
    scores = jnp.concatenate(
        [scores[c * BLK : (c + 1) * BLK, :] + marks[c : c + 1, :] for c in range(CAND)], axis=0
    )
    top = jnp.max(scores, axis=0, keepdims=True)
    probs = jnp.exp2(scores - top).astype(jnp.bfloat16)
    vals = []
    for a in range(4):
        v = [vd[picks[a][c]] for c in range(CAND)]
        vals.append(
            jnp.concatenate(
                [jnp.where(low, v[2 * g], v[2 * g + 1]) for g in range(CAND // 2)], axis=1
            )
        )
    vals.append(jnp.ones((16, CAND * BLK), jnp.bfloat16))
    got = dot(jnp.concatenate(vals, axis=0), probs)
    num = jnp.concatenate(
        [
            jnp.where(low, got[0:64, :LANES], got[64:128, :LANES]),
            jnp.where(low, got[128:192, LANES:], got[192:256, LANES:]),
        ],
        axis=1,
    )
    out = (num / got[256:257, :]).astype(jnp.bfloat16)
    here = quad * 4 + at
    for g in range(2):
        f = fd[g]
        out = jnp.where(here == glob[0, g], jnp.concatenate([f, f], axis=1), out)
    return out


VM = pl.BlockSpec(memory_space=pltpu.VMEM)
SM = pl.BlockSpec(memory_space=pltpu.SMEM)
HB = pl.BlockSpec(memory_space=pltpu.HBM)

NY = 4
NZ = 8
GROUP = 4


def offset(i, near):
    a = i // NY
    step = ((a + 1) // 2) * (1 - 2 * lax.rem(a, 2))
    far = NZ // 2 + step
    b = lax.rem(a + 1, NZ)
    close = NZ + ((b + 1) // 2) * (2 * lax.rem(b, 2) - 1)
    return lax.rem(i + 1, NY), (lax.rem(close, NZ) if near else far)


def target(me, i, near):
    dy, dz = offset(i, near)
    return lax.rem(me // NZ + dy, NY) * NZ + lax.rem(lax.rem(me, NZ) + dz, NZ)


def source(me, i, near):
    dy, dz = offset(i, near)
    return lax.rem(me // NZ + NY - dy, NY) * NZ + lax.rem(lax.rem(me, NZ) + NZ - dz, NZ)


def loop(first, last, f):
    def body(i, c):
        f(i)
        return c

    lax.fori_loop(first, last, body, 0)


def layer_kernel(
    glob, rand_hbm, q, k, v, w, out,
    rand, bias, qr, kr, vr, kd, vd, fd, qg, held, probs, top, full, ob, att, wr, lhs, total,
    sent, got, w_sent, w_got, own,
):
    devices, _, width = qr.shape
    parts = wr.shape[0] // w.shape[0]
    me = lax.axis_index("seq")
    dp = lax.axis_index("dp")
    barrier = pltpu.get_barrier_semaphore()

    def hello(axis, size, at):
        def one(i):
            pl.semaphore_signal(
                barrier, 1, device_id={axis: lax.rem(at + i, size)}, device_id_type=MESH
            )

        loop(1, size, one)

    hello("seq", devices, me)
    hello("dp", parts, dp)
    pl.semaphore_wait(barrier, devices - 1 + parts - 1)

    def remote(t, i, src, dst, to, from_):
        return pltpu.make_async_remote_copy(
            src_ref=src,
            dst_ref=dst,
            send_sem=sent.at[t, i],
            recv_sem=got.at[t, from_],
            device_id={"seq": to},
            device_id_type=MESH,
        )

    pairs = [(q, qr), (k, kr), (v, vr)]

    def send(t, i):
        to = target(me, i, True)
        return remote(t, i, pairs[t][0].at[to], pairs[t][1].at[me], to, me)

    def arrive(t, i):
        s = source(me, i, True)
        remote(t, i, pairs[t][0].at[s], pairs[t][1].at[s], s, s).wait_recv()

    def send_w(i, at):
        to = lax.rem(dp + i, parts)
        return pltpu.make_async_remote_copy(
            src_ref=w,
            dst_ref=wr.at[pl.ds(at * w.shape[0], w.shape[0])],
            send_sem=w_sent.at[i],
            recv_sem=w_got.at[i],
            device_id={"dp": to},
            device_id_type=MESH,
        )

    copies = [pltpu.make_async_copy(a.at[me], b.at[me], own.at[t]) for t, (a, b) in enumerate(pairs)]
    table = pltpu.make_async_copy(rand_hbm, rand, own.at[4])
    table.start()
    copies.append(
        pltpu.make_async_copy(w, wr.at[pl.ds(dp * w.shape[0], w.shape[0])], own.at[3])
    )
    for t in range(3):
        loop(0, devices - 1, lambda i: send(t, i).start())
        copies[t].start()
        if t == 0:
            loop(1, parts, lambda i: send_w(i, dp).start())
            copies[3].start()

    qg[...] = jnp.zeros(qg.shape, qg.dtype)
    top[...] = jnp.full(top.shape, -jnp.inf, jnp.float32)
    full[...] = jnp.zeros(full.shape, jnp.float32)

    def take(t, f):
        copies[t].wait()

        def one(i):
            @pl.when(i < devices - 1)
            def _():
                arrive(t, i)

            f(source(me, i, True))

        loop(0, devices, one)

    table.wait()

    def first(s):
        for h in range(width // QUAD):
            mark_quad(s * (width // QUAD) + h, kd.shape[0], bias, rand, glob)
        take_query(s, qr.at[s], qg, glob)

    take(0, first)
    take(1, lambda s: take_key(s, kr.at[s], kd, qg, held, top))
    best = top_of(top)
    loop(0, devices, lambda s: weigh(s, held, best, probs))
    take(2, lambda s: take_value(s, vr.at[s], vd, probs, full))
    finish_full(full, fd)

    def send_o(i):
        to = target(me, i, False)
        return remote(3, i, ob.at[i], att.at[me], to, me)

    def chunk(i):
        d = target(me, i, False)
        for h in range(width // QUAD):
            cols = slice(h * QUAD, (h + 1) * QUAD)
            ob[i, :, cols] = attend_quad(
                d * (width // QUAD) + h, qr[d, :, cols], kd, vd, fd, rand, bias, glob
            )

        @pl.when(i > 0)
        def _():
            send_o(i - 1).start()

    loop(0, devices, chunk)
    att[me] = ob[devices - 1]
    for t in range(3):
        loop(0, devices - 1, lambda i: send(t, i).wait_send())
    copies[3].wait()
    loop(1, parts, lambda i: send_w(i, lax.rem(dp + parts - i, parts)).wait_recv())

    groups = devices // GROUP

    def project(g, step):
        heads = [source(me, g * GROUP + j, False) for j in range(GROUP)]
        for j in range(GROUP):
            if not (not isinstance(g, jax.Array) and g == groups - 1 and j == GROUP - 1):
                s = heads[j]
                remote(3, g * GROUP + j, ob.at[j], att.at[s], s, s).wait_recv()
        lhs[...] = jnp.concatenate([att[s] for s in heads], axis=0).T

        def tile(n):
            cols = pl.ds(pl.multiple_of(n * QUAD, QUAD), QUAD)
            part = dot(lhs[...], jnp.concatenate([wr[h, :, cols] for h in heads], axis=0))
            if step == 0:
                total[:, cols] = part
            elif step == 1:
                total[:, cols] += part
            else:
                out[:, cols] = (total[:, cols] + part).astype(jnp.bfloat16)

        loop(0, out.shape[1] // QUAD, tile)

    project(0, 0)
    loop(1, 3, lambda g: project(g, 1))
    project(groups - 1, 1)
    loop(3, groups - 2, lambda g: project(g, 1))
    project(groups - 2, 2)

    loop(0, devices - 1, lambda i: send_o(i).wait_send())
    loop(1, parts, lambda i: send_w(i, dp).wait_send())


def layer(glob, rand, q, k, v, w, parts):
    devices, _, width = q.shape
    blocks = devices * width // BLK
    columns = w.shape[2]
    bf = jnp.bfloat16
    dma = pltpu.SemaphoreType.DMA
    return pl.pallas_call(
        layer_kernel,
        out_shape=pltpu.VMEM((width, columns), bf),
        in_specs=[SM, HB, HB, HB, HB, HB],
        out_specs=VM,
        scratch_shapes=[
            pltpu.SMEM(rand.shape, jnp.int32),
            pltpu.VMEM((blocks // 4, CAND, QUAD), jnp.float32),
            pltpu.VMEM((devices, HD, width), bf),
            pltpu.VMEM((devices, HD, width), bf),
            pltpu.VMEM((devices, HD, width), bf),
            pltpu.VMEM((blocks, BLK, LANES), bf),
            pltpu.VMEM((blocks, HD, LANES), bf),
            pltpu.VMEM((2, HD, LANES), bf),
            pltpu.VMEM((HD, LANES), bf),
            pltpu.VMEM((devices, width // 2, 2 * LANES), jnp.float32),
            pltpu.VMEM((devices, width // 2, 2 * LANES), bf),
            pltpu.VMEM((8, 2 * LANES), jnp.float32),
            pltpu.VMEM((2 * HD + 16, 2 * LANES), jnp.float32),
            pltpu.VMEM((devices, HD, width), bf),
            pltpu.VMEM((devices, HD, width), bf),
            pltpu.VMEM((w.shape[0] * parts, HD, columns), bf),
            pltpu.VMEM((width, GROUP * HD), bf),
            pltpu.VMEM((width, columns), jnp.float32),
            dma((4, devices)),
            dma((4, devices)),
            dma((parts,)),
            dma((parts,)),
            dma((5,)),
        ],
        compiler_params=pltpu.CompilerParams(
            collective_id=0, has_side_effects=True, vmem_limit_bytes=54 << 20
        ),
    )(glob, rand, q, k, v, w)


def local(queries, keys, values, random_blocks, global_blocks, out_weight):
    width = queries.shape[2]
    q, k, v = (x[0].reshape(-1, HD, width) for x in (queries, keys, values))
    w = out_weight.reshape(-1, HD, out_weight.shape[1])
    parts = lax.axis_size("dp")
    return layer(global_blocks, random_blocks.transpose(0, 3, 1, 2)[0], q, k, v, w, parts)[None]


def solution(mesh):
    in_specs = (
        P("dp", None, "seq"),
        P("dp", None, "seq"),
        P("dp", None, "seq"),
        P("dp", "seq", None, None),
        P("dp", None),
        P("dp", None),
    )
    out_specs = P("dp", "seq", None)
    return jax.shard_map(local, mesh=mesh, in_specs=in_specs, out_specs=out_specs, check_vma=False)
```

```python
import functools

import jax
import jax.numpy as jnp
from jax import lax
from jax.experimental import pallas as pl
from jax.experimental.pallas import tpu as pltpu
from jax.sharding import PartitionSpec as P

HD = 64
BLK = 64
LANES = 128
CAND = 8
QUAD = 4 * BLK
SCALE = HD ** (-0.5) * 1.4426950408889634
MESH = pl.DeviceIdType.MESH


def dot(a, b):
    return lax.dot_general(a, b, (((1,), (0,)), ((), ())), preferred_element_type=jnp.float32)


def lane(shape):
    return lax.broadcasted_iota(jnp.int32, shape, len(shape) - 1)


def low_half(rows):
    return lane((rows, LANES)) < BLK


def swap(x):
    return jnp.concatenate([x[:, BLK:], x[:, :BLK]], axis=1)


def candidates(block, blocks, rand, glob):
    return [
        jnp.maximum(block - 1, 0),
        block,
        jnp.minimum(block + 1, blocks - 1),
        glob[0, 0],
        glob[0, 1],
    ] + [rand[r, 0, block] for r in range(CAND - 5)]


def mark_quad(quad, blocks, bias, rand, glob):
    at = lane((1, QUAD)) // BLK
    block = quad * 4 + at
    cand = [jnp.maximum(block - 1, 0), block, jnp.minimum(block + 1, blocks - 1)]
    cand += [jnp.full((1, QUAD), glob[0, g], jnp.int32) for g in range(2)]
    for r in range(CAND - 5):
        x = [rand[r, 0, quad * 4 + a] for a in range(4)]
        cand.append(
            jnp.where(at == 0, x[0], jnp.where(at == 1, x[1], jnp.where(at == 2, x[2], x[3])))
        )
    marks = [
        jnp.where(block == 0, -jnp.inf, 0.0),
        jnp.zeros((1, QUAD), jnp.float32),
        jnp.where(block == blocks - 1, -jnp.inf, 0.0),
    ]
    for c in range(3, CAND):
        seen = cand[c] == cand[0]
        for e in range(1, c):
            seen = seen | (cand[c] == cand[e])
        marks.append(jnp.where(seen, -jnp.inf, 0.0))
    for c in range(CAND):
        bias[quad, c : c + 1, :] = marks[c].astype(jnp.float32)


def take_query(s, q, qg, glob):
    at = lane((HD, LANES))
    want = jnp.where(at < BLK, glob[0, 0], glob[0, 1])
    kept = qg[...]
    for i in range(q.shape[1] // LANES):
        x = q[:, i * LANES : (i + 1) * LANES]
        first = s * (q.shape[1] // BLK) + 2 * i
        here = first + jnp.where(at < BLK, 0, 1)
        there = first + jnp.where(at < BLK, 1, 0)
        kept = jnp.where(here == want, x, jnp.where(there == want, swap(x), kept))
    qg[...] = kept


def take_key(s, k, kd, qg, held, top):
    per = k.shape[1] // BLK
    tokens = jnp.concatenate([k[...], k[...]], axis=0).T
    for i in range(per):
        kd[s * per + i] = tokens[i * BLK : (i + 1) * BLK, :]
    half = k.shape[1] // 2
    pairs = jnp.where(low_half(half), tokens[:half, :], tokens[half:, :])
    g = qg[...]
    zero = jnp.zeros_like(g)
    weights = jnp.concatenate(
        [jnp.concatenate([g, zero], axis=1), jnp.concatenate([zero, g], axis=1)], axis=0
    )
    scores = dot(pairs, weights) * SCALE
    held[s] = scores
    best = top[...]
    for r in range(half // 8):
        best = jnp.maximum(best, scores[r * 8 : (r + 1) * 8, :])
    top[...] = best


def top_of(top):
    best = jnp.max(top[...], axis=0, keepdims=True)
    best = jnp.maximum(best[:, :LANES], best[:, LANES:])
    return jnp.concatenate([best, best], axis=1)


def weigh(s, held, best, probs):
    probs[s] = jnp.exp2(held[s] - best).astype(jnp.bfloat16)


def take_value(s, v, vd, probs, full):
    per = v.shape[1] // BLK
    low = low_half(HD)
    for i in range(per // 2):
        x = v[:, i * LANES : (i + 1) * LANES]
        y = swap(x)
        vd[s * per + 2 * i] = jnp.where(low, x, y)
        vd[s * per + 2 * i + 1] = jnp.where(low, y, x)
    half = v.shape[1] // 2
    ones = jnp.ones((16, half), jnp.bfloat16)
    lhs = jnp.concatenate([v[:, :half], v[:, half:], ones], axis=0)
    full[...] += dot(lhs, probs[s])


def finish_full(full, fd):
    num = full[:HD, :LANES] + full[HD : 2 * HD, LANES:]
    row = full[2 * HD : 2 * HD + 1, :]
    out = (num / (row[:, :LANES] + row[:, LANES:])).astype(jnp.bfloat16)
    low = low_half(HD)
    other = swap(out)
    fd[0] = jnp.where(low, out, other)
    fd[1] = jnp.where(low, other, out)


def attend_quad(quad, qq, kd, vd, fd, rand, bias, glob):
    low = low_half(BLK)
    at = lane((HD, QUAD)) // BLK
    zero = jnp.zeros_like(qq)
    weights = jnp.concatenate([jnp.where(at == a, qq, zero) for a in range(4)], axis=0)
    picks = [candidates(quad * 4 + a, kd.shape[0], rand, glob) for a in range(4)]
    keys = []
    for c in range(CAND):
        k = [kd[picks[a][c]] for a in range(4)]
        keys.append(
            jnp.concatenate([jnp.where(low, k[0], k[1]), jnp.where(low, k[2], k[3])], axis=1)
        )
    scores = dot(jnp.concatenate(keys, axis=0), weights) * SCALE
    marks = bias[quad]
    scores = jnp.concatenate(
        [scores[c * BLK : (c + 1) * BLK, :] + marks[c : c + 1, :] for c in range(CAND)], axis=0
    )
    top = jnp.max(scores, axis=0, keepdims=True)
    probs = jnp.exp2(scores - top).astype(jnp.bfloat16)
    vals = []
    for a in range(4):
        v = [vd[picks[a][c]] for c in range(CAND)]
        vals.append(
            jnp.concatenate(
                [jnp.where(low, v[2 * g], v[2 * g + 1]) for g in range(CAND // 2)], axis=1
            )
        )
    vals.append(jnp.ones((16, CAND * BLK), jnp.bfloat16))
    got = dot(jnp.concatenate(vals, axis=0), probs)
    num = jnp.concatenate(
        [
            jnp.where(low, got[0:64, :LANES], got[64:128, :LANES]),
            jnp.where(low, got[128:192, LANES:], got[192:256, LANES:]),
        ],
        axis=1,
    )
    out = (num / got[256:257, :]).astype(jnp.bfloat16)
    here = quad * 4 + at
    for g in range(2):
        f = fd[g]
        out = jnp.where(here == glob[0, g], jnp.concatenate([f, f], axis=1), out)
    return out


VM = pl.BlockSpec(memory_space=pltpu.VMEM)
SM = pl.BlockSpec(memory_space=pltpu.SMEM)
HB = pl.BlockSpec(memory_space=pltpu.HBM)

NY = 4
NZ = 8
GROUP = 4


def offset(i, near):
    a = i // NY
    step = ((a + 1) // 2) * (1 - 2 * lax.rem(a, 2))
    far = NZ // 2 + step
    b = lax.rem(a + 1, NZ)
    close = NZ + ((b + 1) // 2) * (2 * lax.rem(b, 2) - 1)
    return lax.rem(i + 1, NY), (lax.rem(close, NZ) if near else far)


def target(me, i, near):
    dy, dz = offset(i, near)
    return lax.rem(me // NZ + dy, NY) * NZ + lax.rem(lax.rem(me, NZ) + dz, NZ)


def source(me, i, near):
    dy, dz = offset(i, near)
    return lax.rem(me // NZ + NY - dy, NY) * NZ + lax.rem(lax.rem(me, NZ) + NZ - dz, NZ)


def loop(first, last, f):
    def body(i, c):
        f(i)
        return c

    lax.fori_loop(first, last, body, 0)


def layer_kernel(
    glob, rand_hbm, q, k, v, w, out,
    rand, bias, qr, kr, vr, kd, vd, fd, qg, held, probs, top, full, ob, att, wr, lhs, total,
    sent, got, w_sent, w_got, own,
):
    devices, _, width = qr.shape
    parts = wr.shape[0] // w.shape[0]
    me = lax.axis_index("seq")
    dp = lax.axis_index("dp")
    barrier = pltpu.get_barrier_semaphore()

    def hello(axis, size, at):
        def one(i):
            pl.semaphore_signal(
                barrier, 1, device_id={axis: lax.rem(at + i, size)}, device_id_type=MESH
            )

        loop(1, size, one)

    hello("seq", devices, me)
    hello("dp", parts, dp)
    pl.semaphore_wait(barrier, devices - 1 + parts - 1)

    def remote(t, i, src, dst, to, from_):
        return pltpu.make_async_remote_copy(
            src_ref=src,
            dst_ref=dst,
            send_sem=sent.at[t, i],
            recv_sem=got.at[t, from_],
            device_id={"seq": to},
            device_id_type=MESH,
        )

    pairs = [(q, qr), (k, kr), (v, vr)]

    def send(t, i):
        to = target(me, i, True)
        return remote(t, i, pairs[t][0].at[to], pairs[t][1].at[me], to, me)

    def arrive(t, i):
        s = source(me, i, True)
        remote(t, i, pairs[t][0].at[s], pairs[t][1].at[s], s, s).wait_recv()

    def send_w(i, at):
        to = lax.rem(dp + i, parts)
        return pltpu.make_async_remote_copy(
            src_ref=w,
            dst_ref=wr.at[pl.ds(at * w.shape[0], w.shape[0])],
            send_sem=w_sent.at[i],
            recv_sem=w_got.at[i],
            device_id={"dp": to},
            device_id_type=MESH,
        )

    copies = [pltpu.make_async_copy(a.at[me], b.at[me], own.at[t]) for t, (a, b) in enumerate(pairs)]
    table = pltpu.make_async_copy(rand_hbm, rand, own.at[4])
    table.start()
    copies.append(
        pltpu.make_async_copy(w, wr.at[pl.ds(dp * w.shape[0], w.shape[0])], own.at[3])
    )
    for t in range(3):
        loop(0, devices - 1, lambda i: send(t, i).start())
        copies[t].start()
        if t == 2:
            loop(1, parts, lambda i: send_w(i, dp).start())
            copies[3].start()

    qg[...] = jnp.zeros(qg.shape, qg.dtype)
    top[...] = jnp.full(top.shape, -jnp.inf, jnp.float32)
    full[...] = jnp.zeros(full.shape, jnp.float32)

    def take(t, f):
        copies[t].wait()

        def one(i):
            @pl.when(i < devices - 1)
            def _():
                arrive(t, i)

            f(source(me, i, True))

        loop(0, devices, one)

    table.wait()

    def first(s):
        for h in range(width // QUAD):
            mark_quad(s * (width // QUAD) + h, kd.shape[0], bias, rand, glob)
        take_query(s, qr.at[s], qg, glob)

    take(0, first)
    take(1, lambda s: take_key(s, kr.at[s], kd, qg, held, top))
    best = top_of(top)
    loop(0, devices, lambda s: weigh(s, held, best, probs))
    take(2, lambda s: take_value(s, vr.at[s], vd, probs, full))
    finish_full(full, fd)

    def send_o(i):
        to = target(me, i, False)
        return remote(3, i, ob.at[i], att.at[me], to, me)

    def chunk(i):
        d = target(me, i, False)
        for h in range(width // QUAD):
            cols = slice(h * QUAD, (h + 1) * QUAD)
            ob[i, :, cols] = attend_quad(
                d * (width // QUAD) + h, qr[d, :, cols], kd, vd, fd, rand, bias, glob
            )

        @pl.when(i > 0)
        def _():
            send_o(i - 1).start()

    loop(0, devices, chunk)
    att[me] = ob[devices - 1]
    for t in range(3):
        loop(0, devices - 1, lambda i: send(t, i).wait_send())
    copies[3].wait()
    loop(1, parts, lambda i: send_w(i, lax.rem(dp + parts - i, parts)).wait_recv())

    groups = devices // GROUP

    def project(g, step):
        heads = [source(me, g * GROUP + j, False) for j in range(GROUP)]
        for j in range(GROUP):
            if not (not isinstance(g, jax.Array) and g == groups - 1 and j == GROUP - 1):
                s = heads[j]
                remote(3, g * GROUP + j, ob.at[j], att.at[s], s, s).wait_recv()
        lhs[...] = jnp.concatenate([att[s] for s in heads], axis=0).T

        def tile(n):
            cols = pl.ds(pl.multiple_of(n * QUAD, QUAD), QUAD)
            part = dot(lhs[...], jnp.concatenate([wr[h, :, cols] for h in heads], axis=0))
            if step == 0:
                total[:, cols] = part
            elif step == 1:
                total[:, cols] += part
            else:
                out[:, cols] = (total[:, cols] + part).astype(jnp.bfloat16)

        loop(0, out.shape[1] // QUAD, tile)

    project(0, 0)
    loop(1, 3, lambda g: project(g, 1))
    project(groups - 1, 1)
    loop(3, groups - 2, lambda g: project(g, 1))
    project(groups - 2, 2)

    loop(0, devices - 1, lambda i: send_o(i).wait_send())
    loop(1, parts, lambda i: send_w(i, dp).wait_send())


def layer(glob, rand, q, k, v, w, parts):
    devices, _, width = q.shape
    blocks = devices * width // BLK
    columns = w.shape[2]
    bf = jnp.bfloat16
    dma = pltpu.SemaphoreType.DMA
    return pl.pallas_call(
        layer_kernel,
        out_shape=pltpu.VMEM((width, columns), bf),
        in_specs=[SM, HB, HB, HB, HB, HB],
        out_specs=VM,
        scratch_shapes=[
            pltpu.SMEM(rand.shape, jnp.int32),
            pltpu.VMEM((blocks // 4, CAND, QUAD), jnp.float32),
            pltpu.VMEM((devices, HD, width), bf),
            pltpu.VMEM((devices, HD, width), bf),
            pltpu.VMEM((devices, HD, width), bf),
            pltpu.VMEM((blocks, BLK, LANES), bf),
            pltpu.VMEM((blocks, HD, LANES), bf),
            pltpu.VMEM((2, HD, LANES), bf),
            pltpu.VMEM((HD, LANES), bf),
            pltpu.VMEM((devices, width // 2, 2 * LANES), jnp.float32),
            pltpu.VMEM((devices, width // 2, 2 * LANES), bf),
            pltpu.VMEM((8, 2 * LANES), jnp.float32),
            pltpu.VMEM((2 * HD + 16, 2 * LANES), jnp.float32),
            pltpu.VMEM((devices, HD, width), bf),
            pltpu.VMEM((devices, HD, width), bf),
            pltpu.VMEM((w.shape[0] * parts, HD, columns), bf),
            pltpu.VMEM((width, GROUP * HD), bf),
            pltpu.VMEM((width, columns), jnp.float32),
            dma((4, devices)),
            dma((4, devices)),
            dma((parts,)),
            dma((parts,)),
            dma((5,)),
        ],
        compiler_params=pltpu.CompilerParams(
            collective_id=0, has_side_effects=True, vmem_limit_bytes=54 << 20
        ),
    )(glob, rand, q, k, v, w)


def local(queries, keys, values, random_blocks, global_blocks, out_weight):
    width = queries.shape[2]
    q, k, v = (x[0].reshape(-1, HD, width) for x in (queries, keys, values))
    w = out_weight.reshape(-1, HD, out_weight.shape[1])
    parts = lax.axis_size("dp")
    return layer(global_blocks, random_blocks.transpose(0, 3, 1, 2)[0], q, k, v, w, parts)[None]


def solution(mesh):
    in_specs = (
        P("dp", None, "seq"),
        P("dp", None, "seq"),
        P("dp", None, "seq"),
        P("dp", "seq", None, None),
        P("dp", None),
        P("dp", None),
    )
    out_specs = P("dp", "seq", None)
    return jax.shard_map(local, mesh=mesh, in_specs=in_specs, out_specs=out_specs, check_vma=False)
```
